32 devices in a mesh: dp: 8 (over z, y), expert: 4 (over x, core).
Axes of the slice: x: 2, y: 2, z: 4, core: 2. Of those that a mesh axis runs over, the one named last changes fastest.
Arguments:
- tokens: bfloat16 [4096, 1024], P(('dp', 'expert')), may hold values from -6 to 6
- cotangent: bfloat16 [4096, 1024], P(('dp', 'expert')), may hold values from -6 to 6
- expert_ids: int32 [4096, 2], P(('dp', 'expert')), may hold values from 0 to 3, all different within a row; in each aligned block of 128 rows (0 to 127, 128 to 255, ...) at most 128 rows name the same one
- gate_weights: float32 [4096, 2], P(('dp', 'expert')), may hold values from 0.05 to 1
- w_gate: bfloat16 [4, 384, 1024], P('expert'), may hold values from -0.1875 to 0.1875
- w_up: bfloat16 [4, 384, 1024], P('expert'), may hold values from -0.1875 to 0.1875
- w_down: bfloat16 [4, 384, 1024], P('expert'), may hold values from -0.3125 to 0.3125
Outputs:
- layer_out: bfloat16 [4096, 1024], P(('dp', 'expert'))
- grad_tokens: bfloat16 [4096, 1024], P(('dp', 'expert'))
- grad_up: float32 [4, 384, 1024], P('expert', 'dp')
- grad_down: float32 [4, 384, 1024], P('expert', 'dp')
The draws below stay inside these ranges and needn't reach their ends.
Inputs may be any that keep to these rules, and one draw needn't show every extreme that they name: `expert_ids`: each row names 2 different experts. Among the 128 rows of one device no expert is named more than 128 times, and in every draw some expert is named exactly 128 times by the rows of some device.
All inputs are finite; a program needn't handle non-finite values.
Results may differ from the reference program's by a relative error of at most 0.0065.
Values may be sent and summed in bfloat16 or wider, within the bound.
A program may use at most 64 MiB of HBM per device.

```python
import math
import jax
import jax.numpy as jnp
import numpy as np
from jax import lax

D = 1024
H = 384
TOP = 2
TOK_DEV = 128
EXPERTS = 4
CAP = 128
TOKENS = 4096


def level_of(stream_key, extent, shards, low, top_value):
    level = 1.0
    for position, blocks in shards:
        steps = jax.random.uniform(jax.random.fold_in(jax.random.fold_in(stream_key, 6), position), (blocks,), jnp.float32, low / len(shards), top_value / len(shards))
        level = level * jnp.repeat(jnp.exp(steps), extent[position] // blocks).reshape((-1,) + (1,) * (len(extent) - 1 - position))
    return level


def routed_block(own_key, own, number, rows, amount, top, reach, slope):
    ranking = jax.random.permutation(own_key, amount)
    heavy_load, common = shares(amount, rows * top, reach, slope, True), shares(amount, rows * top, reach, slope, False)
    places = jnp.arange(amount)

    def named(sizes, offset_by):
        used = int((sizes > 0).sum())
        fixed = max(1, used // 4)
        moved = fixed + (places - fixed + offset_by * (used - fixed)) % max(1, amount - fixed)
        return jnp.zeros((amount,), jnp.int32).at[ranking[jnp.where(places < fixed, places, moved)]].set(jnp.asarray(sizes, jnp.int32))

    sizes = jnp.where(number % 4 == 0, named(heavy_load, number // 4), named(common, number - number // 4 - 1))
    mixed = jax.random.permutation(jax.random.fold_in(own, 3), amount)
    donor, sink = mixed[0:amount // 2 * 2:2], mixed[1:amount // 2 * 2:2]
    room = jnp.minimum(sizes[donor] - 1, reach - sizes[sink]) // 2
    room = jnp.where((donor == ranking[0]) | (sink == ranking[0]) | (sizes[sink] == 0), 0, jnp.maximum(room, 0))
    moved = jax.random.randint(jax.random.fold_in(own, 4), (amount // 2,), 0, 1 << 20) % (room + 1)
    sizes = sizes.at[donor].add(-moved).at[sink].add(moved)
    items = jnp.searchsorted(jnp.cumsum(sizes), jnp.arange(rows * top), side="right").astype(jnp.int32)
    grid = items.reshape(top, rows).T
    grid = grid[jax.random.permutation(jax.random.fold_in(own, 1), rows)]
    offset_by = jax.random.randint(jax.random.fold_in(own, 2), (rows, 1), 0, top)
    return jnp.take_along_axis(grid, (jnp.arange(top)[None, :] + offset_by) % top, axis=1)


def shares(count, total, bound, slope, full):
    weights = [(1 << 20) // math.isqrt(grade ** slope) + 1 for grade in range(1, count + 1)]
    largest = bound if full else min(bound, max(-(-total // count), total * weights[0] // sum(weights)))
    least = 1 if total - largest >= count - 1 else 0
    given, rest = [largest] + [least] * (count - 1), total - largest - least * (count - 1)
    while rest > 0:
        free = [i for i in range(1, count) if given[i] < largest] or [i for i in range(1, count) if given[i] < bound]
        whole, left = sum([weights[i] for i in free]), rest
        for i in free:
            extra = min(bound - given[i], max(1, left * weights[i] // whole), rest)
            given[i] = given[i] + extra
            rest = rest - extra
    return np.array(given)


def normal_values(rng, shape, scale, limit, pieces=(), held_as=jnp.bfloat16):
    result = scale * jax.random.normal(rng, shape, jnp.float32)
    if pieces:
        result = result * level_of(rng, shape, pieces, -0.22, 0.18)
    return jnp.clip(result, -limit, limit).astype(held_as)


def setup_inputs(seed: int = 0) -> dict:
    arg_keys = jax.random.split(jax.random.key(seed), 8)
    tokens = normal_values(arg_keys[0], (TOKENS, D), 1.0, 6.0, ((0, 32),))
    cotangent = normal_values(arg_keys[1], (TOKENS, D), 1.0, 6.0, ((0, 32),))
    expert_ids_keys = jax.random.split(jax.random.fold_in(arg_keys[2], 1), TOKENS // TOK_DEV)
    expert_ids_turns = jax.random.permutation(jax.random.fold_in(arg_keys[2], 3), TOKENS // TOK_DEV)
    expert_ids = jax.vmap(lambda own, number: routed_block(jax.random.fold_in(arg_keys[2], 2), own, number, TOK_DEV, EXPERTS, TOP, CAP, 2))(expert_ids_keys, expert_ids_turns).reshape((TOKENS, TOP))
    gate_weights = jnp.clip(jnp.exp(math.log(1.0) - 2.9957323 * jax.random.uniform(arg_keys[3], (TOKENS, TOP), jnp.float32) ** level_of(arg_keys[3], (TOKENS, TOP), ((0, 32),), -0.2, 0.2)), 0.05, 1.0)
    w_gate = normal_values(arg_keys[4], (EXPERTS, H, D), D ** -0.5, 0.1875, ((0, 4),))
    w_up = normal_values(arg_keys[5], (EXPERTS, H, D), D ** -0.5, 0.1875, ((0, 4),))
    w_down = normal_values(arg_keys[6], (EXPERTS, H, D), H ** -0.5, 0.3125, ((0, 4),))
    return dict(tokens=tokens, cotangent=cotangent, expert_ids=expert_ids, gate_weights=gate_weights, w_gate=w_gate, w_up=w_up, w_down=w_down)


def expert_block(block_tokens, grad_out, weight_gate, weight_up, weight_down):
    gate_pre = jnp.dot(block_tokens, weight_gate.T, preferred_element_type=jnp.float32)
    up_pre = jnp.dot(block_tokens, weight_up.T, preferred_element_type=jnp.float32)
    gate_sig = jax.nn.sigmoid(gate_pre)
    hidden = (gate_pre * gate_sig * up_pre).astype(jnp.bfloat16)
    expert_out = jnp.dot(hidden, weight_down, preferred_element_type=jnp.float32).astype(jnp.bfloat16)
    grad_hidden = jnp.dot(grad_out, weight_down.T, preferred_element_type=jnp.float32)
    grad_up_pre = (grad_hidden * gate_pre * gate_sig).astype(jnp.bfloat16)
    grad_gate_pre = (grad_hidden * up_pre * gate_sig * (1.0 + gate_pre * (1.0 - gate_sig))).astype(jnp.bfloat16)
    grad_input = (jnp.dot(grad_gate_pre, weight_gate, preferred_element_type=jnp.float32)
                  + jnp.dot(grad_up_pre, weight_up, preferred_element_type=jnp.float32)).astype(jnp.bfloat16)
    grad_upper = jnp.dot(grad_up_pre.T, block_tokens, preferred_element_type=jnp.float32)
    grad_lower = jnp.dot(hidden.T, grad_out, preferred_element_type=jnp.float32)
    return expert_out, grad_input, grad_upper, grad_lower


def reference(tokens, cotangent, expert_ids, gate_weights, w_gate, w_up, w_down):
    block_rows = 1024
    experts = w_gate.shape[0]
    top_count = expert_ids.shape[1]
    flat_ids = expert_ids.reshape(-1).astype(jnp.int32)
    assignments = flat_ids.shape[0]
    sorted_order = jnp.argsort(flat_ids, stable=True).astype(jnp.int32)
    expert_range = jnp.arange(experts, dtype=jnp.int32)
    counts = jnp.sum((flat_ids[:, None] == expert_range[None, :]).astype(jnp.int32), axis=0).astype(jnp.int32)
    starts = (jnp.cumsum(counts) - counts).astype(jnp.int32)
    padded = ((counts + block_rows - 1) // block_rows * block_rows).astype(jnp.int32)
    pad_starts = (jnp.cumsum(padded) - padded).astype(jnp.int32)
    sorted_ids = flat_ids[sorted_order]
    slot_rank = jnp.arange(assignments, dtype=jnp.int32) - starts[sorted_ids]
    padded_pos = (pad_starts[sorted_ids] + slot_rank).astype(jnp.int32)
    block_count = assignments // block_rows + experts + 1
    row_table = jnp.full((block_count * block_rows,), -1, jnp.int32).at[padded_pos].set(sorted_order)
    block_first = jnp.arange(block_count, dtype=jnp.int32) * block_rows
    block_ends = pad_starts + padded
    block_expert = jnp.minimum(jnp.sum((block_ends[None, :] <= block_first[:, None]).astype(jnp.int32), axis=1),
                               experts - 1).astype(jnp.int32)
    flat_gates = gate_weights.reshape(-1).astype(jnp.float32)

    def step(running, scanned):
        y_acc, dx_acc, g_upper, g_lower = running
        row_ids, expert = scanned
        filled = row_ids >= 0
        clipped = jnp.maximum(row_ids, 0)
        token_rows = (clipped // top_count).astype(jnp.int32)
        block_tokens = jnp.where(filled[:, None], tokens[token_rows], jnp.zeros((), tokens.dtype))
        block_gates = jnp.where(filled, flat_gates[clipped], jnp.zeros((), jnp.float32))
        grad_out = (block_gates[:, None] * cotangent[token_rows].astype(jnp.float32)).astype(jnp.bfloat16)
        results = expert_block(block_tokens, grad_out, w_gate[expert], w_up[expert], w_down[expert])
        y_acc = y_acc.at[token_rows].add(block_gates[:, None] * results[0].astype(jnp.float32))
        dx_acc = dx_acc.at[token_rows].add(results[1].astype(jnp.float32))
        g_upper = g_upper.at[expert].add(results[2])
        g_lower = g_lower.at[expert].add(results[3])
        return (y_acc, dx_acc, g_upper, g_lower), None

    start_state = (jnp.zeros(tokens.shape, jnp.float32), jnp.zeros(tokens.shape, jnp.float32),
                   jnp.zeros(w_gate.shape, jnp.float32), jnp.zeros(w_gate.shape, jnp.float32))
    final_state, unused = lax.scan(step, start_state, (row_table.reshape(block_count, block_rows), block_expert))
    grad_scale = (TOKENS * TOP / EXPERTS) ** -0.5
    return (final_state[0].astype(jnp.bfloat16), final_state[1].astype(jnp.bfloat16),
            final_state[2] * grad_scale, final_state[3] * grad_scale)
```

```python
import functools

import jax
import jax.numpy as jnp
from jax import lax
from jax.experimental import pallas as pl
from jax.experimental.pallas import tpu as pltpu
from jax.sharding import PartitionSpec as P

MESH = pl.DeviceIdType.MESH
F32 = jnp.float32
BF16 = jnp.bfloat16


def dot_nn(a, b):
    return lax.dot_general(a, b, (((1,), (0,)), ((), ())), preferred_element_type=F32)


def dot_nt(a, b):
    return lax.dot_general(a, b, (((1,), (1,)), ((), ())), preferred_element_type=F32)


def layer_kernel(cfg, tok_hbm, cot_hbm, gates_ref, wg_hbm, wu_hbm, wd_hbm,
                 out_ref, gtok_ref, gup_ref, gdn_ref,
                 wg, wu, wd, xb, cb, gts, gob, hT, guT, silu_s, q_s, ggp_s, gup_s,
                 part, pre, pre_send, ret, gbuf, yrecv, zsend, zrecv,
                 local_sem, xs, xr, ps, pr, rs, rr, ts, tr, qs, qr, us, ur, ys, yr, zs, zr):
    chips, outer, fused, scale = cfg
    T, D = tok_hbm.shape
    H = wg.shape[0]
    R2 = 2 * T
    dp = lax.axis_index("dp")
    ex = lax.axis_index("expert")
    core = lax.rem(ex, 2)
    chip = lax.div(ex, 2)
    partner = (dp, chip * 2 + 1 - core)

    def ahead(d):
        return (dp, lax.rem(chip + d, chips) * 2 + core)

    def behind(d):
        return (dp, lax.rem(chip + chips - d, chips) * 2 + core)

    yi = lax.rem(dp, 2)
    zo = lax.div(dp, 2)
    ypeer = (zo * 2 + 1 - yi, ex)

    def zahead(d):
        return (lax.rem(zo + d, outer) * 2 + yi, ex)

    def remote(src, dst, ssem, rsem, dev):
        return pltpu.make_async_remote_copy(src_ref=src, dst_ref=dst, send_sem=ssem, recv_sem=rsem,
                                            device_id=dev, device_id_type=MESH)

    locals_ = [
        pltpu.make_async_copy(tok_hbm, xb.at[0], local_sem.at[0]),
        pltpu.make_async_copy(wg_hbm.at[0], wg, local_sem.at[1]),
        pltpu.make_async_copy(wu_hbm.at[0], wu, local_sem.at[2]),
        pltpu.make_async_copy(wd_hbm.at[0], wd, local_sem.at[3]),
        pltpu.make_async_copy(cot_hbm, cb.at[0], local_sem.at[4]),
    ]
    for c in locals_:
        c.start()

    peers = [partner] + [ahead(d) for d in range(1, chips)]
    if fused:
        peers = peers + [ypeer] + [zahead(d) for d in range(1, outer)]
    barrier = pltpu.get_barrier_semaphore()
    for dev in peers:
        pl.semaphore_signal(barrier, inc=1, device_id=dev, device_id_type=MESH)
    pl.semaphore_wait(barrier, len(peers))

    pending = []

    def go(c):
        c.start()
        pending.append(c)
        return c

    srcs = [gates_ref, tok_hbm, cot_hbm]
    bufs = [gts, xb, cb]
    xin, pin, rin = {}, {}, {}
    for t in range(3):
        for d in range(1, chips):
            xin[t, d] = go(remote(srcs[t], bufs[t].at[2 * d], xs.at[t, d], xr.at[t, d], ahead(d)))
        if t < 2:
            pin[t] = go(remote(srcs[t], bufs[t].at[1], ps.at[t], pr.at[t], partner))
    pin[2] = go(remote(srcs[2], bufs[2].at[1], ps.at[2], pr.at[2], partner))

    def relay(t):
        for d in range(1, chips):
            xin[t, d].wait_recv()
            rin[t, d] = go(remote(bufs[t].at[2 * d], bufs[t].at[2 * d + 1], rs.at[t, d], rr.at[t, d], partner))

    eye = lax.broadcasted_iota(jnp.int32, (T, T), 0) == lax.broadcasted_iota(jnp.int32, (T, T), 1)

    def gate_col(p):
        cols = []
        for s in (2 * p, 2 * p + 1):
            row = gates_ref[pl.ds(ex, 1), :] if s == 0 else gts[s, pl.ds(ex, 1), :]
            cols.append(jnp.sum(jnp.where(eye, row, 0.0), axis=1, keepdims=True))
        return jnp.concatenate(cols, axis=0)

    def forward(p):
        rows = pl.ds(p * R2, R2)
        x = xb[2 * p:2 * p + 2].reshape(R2, D)
        gp = dot_nt(x, wg[...])
        up = dot_nt(x, wu[...])
        sig = jax.nn.sigmoid(gp)
        silu = gp * sig
        hidden = (silu * up).astype(BF16)
        silu_s[rows, :] = silu
        q_s[rows, :] = up * sig * (1.0 + gp * (1.0 - sig))
        hT[:, rows] = hidden.T
        return hidden

    def forward_out(p, hidden):
        eo = gate_col(p) * dot_nn(hidden, wd[...])
        part[0, 2 * p:2 * p + 2] = eo.astype(BF16).reshape(2, T, D)

    def weighted(p):
        go_ = gate_col(p) * cb[2 * p:2 * p + 2].reshape(R2, D).astype(F32)
        gob[pl.ds(p * R2, R2), :] = go_.astype(BF16)

    def backward(p):
        rows = pl.ds(p * R2, R2)
        gh = dot_nt(gob[rows, :], wd[...])
        gu = (gh * silu_s[rows, :]).astype(BF16)
        gup_s[rows, :] = gu
        ggp_s[rows, :] = (gh * q_s[rows, :]).astype(BF16)
        guT[:, rows] = gu.T

    def backward_in(p):
        rows = pl.ds(p * R2, R2)
        gi = dot_nn(ggp_s[rows, :], wg[...]) + dot_nn(gup_s[rows, :], wu[...])
        part[1, 2 * p:2 * p + 2] = gi.astype(BF16).reshape(2, T, D)

    locals_[0].wait()
    locals_[1].wait()
    locals_[2].wait()
    pin[0].wait_recv()
    pin[1].wait_recv()
    hidden = forward(0)
    locals_[3].wait()
    forward_out(0, hidden)
    tin, qin, uin = {}, {}, {}
    tin[0] = go(remote(part.at[0, 1], ret.at[0, 0], ts.at[0], tr.at[0], partner))
    relay(0)
    locals_[4].wait()
    pin[2].wait_recv()
    weighted(0)
    backward(0)
    relay(1)
    backward_in(0)
    tin[1] = go(remote(part.at[1, 1], ret.at[1, 0], ts.at[1], tr.at[1], partner))

    def hand_over(k):
        for d in range(1, chips):
            qin[k, d] = go(remote(part.at[k, 2 * d + 1], pre.at[k, d], qs.at[k, d], qr.at[k, d], partner))

    def send_back(k):
        for d in range(1, chips):
            qin[k, d].wait_recv()
            pre_send[k, d] = (part[k, 2 * d].astype(F32) + pre[k, d].astype(F32)).astype(BF16)
            uin[k, d] = go(remote(pre_send.at[k, d], ret.at[k, d], us.at[k, d], ur.at[k, d], behind(d)))

    for d in range(1, chips):
        rin[0, d].wait_recv()
        rin[1, d].wait_recv()
        forward_out(d, forward(d))
    hand_over(0)
    relay(2)
    for d in range(1, chips):
        rin[2, d].wait_recv()
        weighted(d)

    yin, zin = {}, {}

    def weight_grad(k, left, right, full_ref):
        tile = 256 if D % 256 == 0 else D
        for n in range(D // tile):
            cols = pl.ds(n * tile, tile)
            g = dot_nn(left[...], right(cols))
            if fused:
                gbuf[k, :, :, :, cols] = g.astype(BF16).reshape(gbuf.shape[1:4] + (tile,))
            else:
                full_ref[:, cols] = g * scale
        if fused:
            for d in list(range(1, outer)) + [0]:
                yin[k, d] = go(remote(gbuf.at[k, lax.rem(zo + d, outer), 1 - yi], yrecv.at[k, d],
                                      ys.at[k, d], yr.at[k, d], ypeer))

    def outer_step(k):
        for d in range(1, outer):
            yin[k, d].wait_recv()
            zsend[k, d] = (gbuf[k, lax.rem(zo + d, outer), yi].astype(F32) + yrecv[k, d].astype(F32)).astype(BF16)
            zin[k, d] = go(remote(zsend.at[k, d], zrecv.at[k, d], zs.at[k, d], zr.at[k, d], zahead(d)))

    def outer_end(k, ref):
        yin[k, 0].wait_recv()
        total = gbuf[k, zo, yi].astype(F32) + yrecv[k, 0].astype(F32)
        for d in range(1, outer):
            zin[k, d].wait_recv()
            total = total + zrecv[k, d].astype(F32)
        ref[...] = total * scale

    weight_grad(0, hT, lambda cols: gob[:, cols], gdn_ref)
    for d in range(1, chips):
        backward(d)
    weight_grad(1, guT, lambda cols: jnp.concatenate([xb[s, :, cols] for s in range(2 * chips)], axis=0), gup_ref)
    send_back(0)
    for d in range(1, chips):
        backward_in(d)
    hand_over(1)
    send_back(1)
    if fused:
        outer_step(0)
        outer_step(1)

    def collect(k, ref):
        total = part[k, 0].astype(F32)
        tin[k].wait_recv()
        total = total + ret[k, 0].astype(F32)
        for d in range(1, chips):
            uin[k, d].wait_recv()
            total = total + ret[k, d].astype(F32)
        ref[...] = total.astype(BF16)

    collect(0, out_ref)
    collect(1, gtok_ref)
    if fused:
        outer_end(0, gdn_ref)
        outer_end(1, gup_ref)
    for c in pending:
        c.wait_send()


def shards(tokens, cotangent, expert_ids, gate_weights, w_gate, w_up, w_down):
    T, D = tokens.shape
    local_experts, H, _ = w_gate.shape
    groups = lax.axis_size("expert")
    dps = lax.axis_size("dp")
    experts = groups * local_experts
    assert local_experts == 1 and groups % 2 == 0
    chips = groups // 2
    piece = H // dps
    fused = dps % 2 == 0 and piece % 16 == 0
    outer = dps // 2 if fused else 1
    top = expert_ids.shape[1]
    scale = (T * dps * groups * top / experts) ** (-0.5)
    erows = -(-experts // 8) * 8
    gates = jnp.sum(
        jnp.where(expert_ids[None, :, :] == jnp.arange(erows, dtype=jnp.int32)[:, None, None],
                  gate_weights[None, :, :], 0.0), axis=2)
    R = groups * T
    grad_shape = (piece, D) if fused else (H, D)
    gp = piece if fused else 16
    vm = pltpu.VMEM
    dma = pltpu.SemaphoreType.DMA
    anyspec = pl.BlockSpec(memory_space=pl.ANY)
    vspec = pl.BlockSpec(memory_space=pltpu.VMEM)
    layer_out, grad_tokens, gup, gdn = pl.pallas_call(
        functools.partial(layer_kernel, (chips, outer, fused, scale)),
        out_shape=(
            jax.ShapeDtypeStruct((T, D), BF16),
            jax.ShapeDtypeStruct((T, D), BF16),
            jax.ShapeDtypeStruct(grad_shape, F32),
            jax.ShapeDtypeStruct(grad_shape, F32),
        ),
        in_specs=[anyspec, anyspec, vspec, anyspec, anyspec, anyspec],
        out_specs=(vspec, vspec, vspec, vspec),
        scratch_shapes=[
            vm((H, D), BF16), vm((H, D), BF16), vm((H, D), BF16),
            vm((groups, T, D), BF16), vm((groups, T, D), BF16), vm((groups, erows, T), F32),
            vm((R, D), BF16), vm((H, R), BF16), vm((H, R), BF16),
            vm((R, H), F32), vm((R, H), F32), vm((R, H), BF16), vm((R, H), BF16),
            vm((2, groups, T, D), BF16), vm((2, chips, T, D), BF16), vm((2, chips, T, D), BF16),
            vm((2, chips, T, D), BF16),
            vm((2, outer, 2, gp, D), BF16), vm((2, outer, gp, D), BF16),
            vm((2, outer, gp, D), BF16), vm((2, outer, gp, D), BF16),
            dma((5,)),
            dma((3, chips)), dma((3, chips)), dma((3,)), dma((3,)), dma((3, chips)), dma((3, chips)),
            dma((2,)), dma((2,)), dma((2, chips)), dma((2, chips)), dma((2, chips)), dma((2, chips)),
            dma((2, outer)), dma((2, outer)), dma((2, outer)), dma((2, outer)),
        ],
        compiler_params=pltpu.CompilerParams(collective_id=0, has_side_effects=True,
                                             vmem_limit_bytes=60 * 1024 * 1024),
        name="moe_layer",
    )(tokens, cotangent, gates, w_gate, w_up, w_down)
    if not fused:
        gup = lax.psum_scatter(gup, "dp", scatter_dimension=0, tiled=True)
        gdn = lax.psum_scatter(gdn, "dp", scatter_dimension=0, tiled=True)
    return layer_out, grad_tokens, gup[None], gdn[None]


def solution(mesh):
    both = P(("dp", "expert"), None)
    weights = P("expert", None, None)
    return jax.shard_map(
        shards,
        mesh=mesh,
        in_specs=(both, both, both, both, weights, weights, weights),
        out_specs=(both, both, P("expert", "dp", None), P("expert", "dp", None)),
        check_vma=False,
    )
```

```python
import functools

import jax
import jax.numpy as jnp
from jax import lax
from jax.experimental import pallas as pl
from jax.experimental.pallas import tpu as pltpu
from jax.sharding import PartitionSpec as P

MESH = pl.DeviceIdType.MESH
F32 = jnp.float32
BF16 = jnp.bfloat16


def dot_nn(a, b):
    return lax.dot_general(a, b, (((1,), (0,)), ((), ())), preferred_element_type=F32)


def dot_nt(a, b):
    return lax.dot_general(a, b, (((1,), (1,)), ((), ())), preferred_element_type=F32)


def layer_kernel(cfg, tok_hbm, cot_hbm, ids_ref, gw_ref, wg_hbm, wu_hbm, wd_hbm,
                 out_ref, gtok_ref, gup_ref, gdn_ref,
                 wg, wu, wd, xb, cb, gates_ref, gts, gob, hT, guT, silu_s, q_s, ggp_s, gup_s,
                 part, pre, pre_send, ret, gbuf, yrecv, zsend, zrecv,
                 local_sem, xs, xr, ps, pr, rs, rr, ts, tr, qs, qr, us, ur, ys, yr, zs, zr):
    chips, outer, fused, scale = cfg
    T, D = tok_hbm.shape
    H = wg.shape[0]
    R2 = 2 * T
    dp = lax.axis_index("dp")
    ex = lax.axis_index("expert")
    core = lax.rem(ex, 2)
    chip = lax.div(ex, 2)
    partner = (dp, chip * 2 + 1 - core)

    def ahead(d):
        return (dp, lax.rem(chip + d, chips) * 2 + core)

    def behind(d):
        return (dp, lax.rem(chip + chips - d, chips) * 2 + core)

    yi = lax.rem(dp, 2)
    zo = lax.div(dp, 2)
    ypeer = (zo * 2 + 1 - yi, ex)

    levels = outer.bit_length() - 1

    def flipped(m):
        z = zo
        for b in range(levels):
            if (m >> b) & 1:
                z = z + (1 << b) * (1 - 2 * lax.rem(lax.div(zo, 1 << b), 2))
        return z

    def remote(src, dst, ssem, rsem, dev):
        return pltpu.make_async_remote_copy(src_ref=src, dst_ref=dst, send_sem=ssem, recv_sem=rsem,
                                            device_id=dev, device_id_type=MESH)

    locals_ = [
        pltpu.make_async_copy(tok_hbm, xb.at[0], local_sem.at[0]),
        pltpu.make_async_copy(wg_hbm.at[0], wg, local_sem.at[1]),
        pltpu.make_async_copy(wu_hbm.at[0], wu, local_sem.at[2]),
        pltpu.make_async_copy(wd_hbm.at[0], wd, local_sem.at[3]),
        pltpu.make_async_copy(cot_hbm, cb.at[0], local_sem.at[4]),
    ]
    for c in locals_:
        c.start()

    ranks = lax.broadcasted_iota(jnp.int32, gates_ref.shape, 0)
    table = jnp.zeros(gates_ref.shape, F32)
    for k in range(ids_ref.shape[0]):
        table = table + jnp.where(ids_ref[pl.ds(k, 1), :] == ranks, gw_ref[pl.ds(k, 1), :], 0.0)
    gates_ref[...] = table

    peers = [partner] + [ahead(d) for d in range(1, chips)]
    if fused:
        peers = peers + [ypeer] + [(flipped(1 << b) * 2 + yi, ex) for b in range(levels)]
    barrier = pltpu.get_barrier_semaphore()
    for dev in peers:
        pl.semaphore_signal(barrier, inc=1, device_id=dev, device_id_type=MESH)
    pl.semaphore_wait(barrier, len(peers))

    pending = []

    def go(c):
        c.start()
        pending.append(c)
        return c

    srcs = [gates_ref, tok_hbm, cot_hbm]
    bufs = [gts, xb, cb]
    xin, pin, rin = {}, {}, {}
    for t in range(3):
        for d in range(1, chips):
            xin[t, d] = go(remote(srcs[t], bufs[t].at[2 * d], xs.at[t, d], xr.at[t, d], ahead(d)))
        if t < 2:
            pin[t] = go(remote(srcs[t], bufs[t].at[1], ps.at[t], pr.at[t], partner))
    pin[2] = go(remote(srcs[2], bufs[2].at[1], ps.at[2], pr.at[2], partner))

    def relay(t):
        for d in range(1, chips):
            xin[t, d].wait_recv()
            rin[t, d] = go(remote(bufs[t].at[2 * d], bufs[t].at[2 * d + 1], rs.at[t, d], rr.at[t, d], partner))

    eye = lax.broadcasted_iota(jnp.int32, (T, T), 0) == lax.broadcasted_iota(jnp.int32, (T, T), 1)

    def gate_col(p):
        cols = []
        for s in (2 * p, 2 * p + 1):
            row = gates_ref[pl.ds(ex, 1), :] if s == 0 else gts[s, pl.ds(ex, 1), :]
            cols.append(jnp.sum(jnp.where(eye, row, 0.0), axis=1, keepdims=True))
        return jnp.concatenate(cols, axis=0)

    def forward(p):
        rows = pl.ds(p * R2, R2)
        x = xb[2 * p:2 * p + 2].reshape(R2, D)
        gp = dot_nt(x, wg[...])
        up = dot_nt(x, wu[...])
        sig = jax.nn.sigmoid(gp)
        silu = gp * sig
        hidden = (silu * up).astype(BF16)
        silu_s[rows, :] = silu
        q_s[rows, :] = up * sig * (1.0 + gp * (1.0 - sig))
        hT[:, rows] = hidden.T
        return hidden

    def forward_out(p, hidden):
        eo = gate_col(p) * dot_nn(hidden, wd[...])
        part[0, 2 * p:2 * p + 2] = eo.astype(BF16).reshape(2, T, D)

    def weighted(p):
        go_ = gate_col(p) * cb[2 * p:2 * p + 2].reshape(R2, D).astype(F32)
        gob[pl.ds(p * R2, R2), :] = go_.astype(BF16)

    def backward(p):
        rows = pl.ds(p * R2, R2)
        gh = dot_nt(gob[rows, :], wd[...])
        gu = (gh * silu_s[rows, :]).astype(BF16)
        gup_s[rows, :] = gu
        ggp_s[rows, :] = (gh * q_s[rows, :]).astype(BF16)
        guT[:, rows] = gu.T

    def backward_in(p):
        rows = pl.ds(p * R2, R2)
        gi = dot_nn(ggp_s[rows, :], wg[...]) + dot_nn(gup_s[rows, :], wu[...])
        part[1, 2 * p:2 * p + 2] = gi.astype(BF16).reshape(2, T, D)

    locals_[0].wait()
    locals_[1].wait()
    locals_[2].wait()
    pin[0].wait_recv()
    pin[1].wait_recv()
    hidden = forward(0)
    locals_[3].wait()
    forward_out(0, hidden)
    tin, qin, uin = {}, {}, {}
    tin[0] = go(remote(part.at[0, 1], ret.at[0, 0], ts.at[0], tr.at[0], partner))
    relay(0)
    locals_[4].wait()
    pin[2].wait_recv()
    weighted(0)
    backward(0)
    relay(1)
    backward_in(0)
    tin[1] = go(remote(part.at[1, 1], ret.at[1, 0], ts.at[1], tr.at[1], partner))

    def hand_over(k):
        for d in range(1, chips):
            qin[k, d] = go(remote(part.at[k, 2 * d + 1], pre.at[k, d], qs.at[k, d], qr.at[k, d], partner))

    def send_back(k):
        for d in range(1, chips):
            qin[k, d].wait_recv()
            pre_send[k, d] = (part[k, 2 * d].astype(F32) + pre[k, d].astype(F32)).astype(BF16)
            uin[k, d] = go(remote(pre_send.at[k, d], ret.at[k, d], us.at[k, d], ur.at[k, d], behind(d)))

    for d in range(1, chips):
        rin[0, d].wait_recv()
        rin[1, d].wait_recv()
        forward_out(d, forward(d))
    hand_over(0)
    relay(2)
    for d in range(1, chips):
        rin[2, d].wait_recv()
        weighted(d)

    yin, zin = {}, {}
    order = sorted(range(outer), key=lambda m: (m & -m) if m else outer)

    def weight_grad(k, left, right, full_ref):
        tile = 256 if D % 256 == 0 else D
        for n in range(D // tile):
            cols = pl.ds(n * tile, tile)
            g = dot_nn(left[...], right(cols))
            if fused:
                gbuf[k, :, :, :, cols] = g.astype(BF16).reshape(gbuf.shape[1:4] + (tile,))
            else:
                full_ref[:, cols] = g * scale
        if fused:
            for m in order:
                yin[k, m] = go(remote(gbuf.at[k, flipped(m), 1 - yi], yrecv.at[k, m],
                                      ys.at[k, m], yr.at[k, m], ypeer))

    def halve(k, b):
        for m in order:
            if (m & -m) == 1 << b:
                total = level_sum(k, m, b)
                zsend[k, m] = total.astype(BF16)
                zin[k, m] = go(remote(zsend.at[k, m], zrecv.at[k, m], zs.at[k, m], zr.at[k, m],
                                      (flipped(1 << b) * 2 + yi, ex)))

    def level_sum(k, m, b):
        yin[k, m].wait_recv()
        total = gbuf[k, flipped(m), yi].astype(F32) + yrecv[k, m].astype(F32)
        for a in range(b):
            zin[k, m + (1 << a)].wait_recv()
            total = total + zrecv[k, m + (1 << a)].astype(F32)
        return total

    def outer_end(k, ref):
        ref[...] = level_sum(k, 0, levels) * scale

    weight_grad(0, hT, lambda cols: gob[:, cols], gdn_ref)
    for d in range(1, chips):
        backward(d)
    weight_grad(1, guT, lambda cols: jnp.concatenate([xb[s, :, cols] for s in range(2 * chips)], axis=0), gup_ref)
    send_back(0)
    for d in range(1, chips):
        backward_in(d)
    hand_over(1)
    if fused and levels > 0:
        halve(0, 0)
    send_back(1)
    if fused:
        for b in range(1, levels):
            halve(0, b)
        for b in range(levels):
            halve(1, b)

    def collect(k, ref):
        total = part[k, 0].astype(F32)
        tin[k].wait_recv()
        total = total + ret[k, 0].astype(F32)
        for d in range(1, chips):
            uin[k, d].wait_recv()
            total = total + ret[k, d].astype(F32)
        ref[...] = total.astype(BF16)

    collect(0, out_ref)
    collect(1, gtok_ref)
    if fused:
        outer_end(0, gdn_ref)
        outer_end(1, gup_ref)
    for c in pending:
        c.wait_send()


def write_out(a, b, c, d, out_a, out_b, out_c, out_d, sem):
    copies = [pltpu.make_async_copy(src, dst, sem.at[i])
              for i, (src, dst) in enumerate([(a, out_a), (b, out_b), (c, out_c), (d, out_d)])]
    for c in copies:
        c.start()
    for c in copies:
        c.wait()


def shards(tokens, cotangent, expert_ids, gate_weights, w_gate, w_up, w_down):
    T, D = tokens.shape
    local_experts, H, _ = w_gate.shape
    groups = lax.axis_size("expert")
    dps = lax.axis_size("dp")
    experts = groups * local_experts
    assert local_experts == 1 and groups % 2 == 0
    chips = groups // 2
    piece = H // dps
    fused = dps % 2 == 0 and piece % 16 == 0 and (dps & (dps - 1)) == 0
    outer = dps // 2 if fused else 1
    top = expert_ids.shape[1]
    scale = (T * dps * groups * top / experts) ** (-0.5)
    erows = -(-experts // 8) * 8
    R = groups * T
    grad_shape = (piece, D) if fused else (H, D)
    gp = piece if fused else 16
    vm = pltpu.VMEM
    dma = pltpu.SemaphoreType.DMA
    anyspec = pl.BlockSpec(memory_space=pl.ANY)
    vspec = pl.BlockSpec(memory_space=pltpu.VMEM)
    layer_out, grad_tokens, gup, gdn = pl.pallas_call(
        functools.partial(layer_kernel, (chips, outer, fused, scale)),
        out_shape=(
            vm((T, D), BF16),
            vm((T, D), BF16),
            vm(grad_shape, F32),
            vm(grad_shape, F32),
        ),
        in_specs=[anyspec, anyspec, vspec, vspec, anyspec, anyspec, anyspec],
        out_specs=(vspec, vspec, vspec, vspec),
        scratch_shapes=[
            vm((H, D), BF16), vm((H, D), BF16), vm((H, D), BF16),
            vm((groups, T, D), BF16), vm((groups, T, D), BF16), vm((erows, T), F32), vm((groups, erows, T), F32),
            vm((R, D), BF16), vm((H, R), BF16), vm((H, R), BF16),
            vm((R, H), F32), vm((R, H), F32), vm((R, H), BF16), vm((R, H), BF16),
            vm((2, groups, T, D), BF16), vm((2, chips, T, D), BF16), vm((2, chips, T, D), BF16),
            vm((2, chips, T, D), BF16),
            vm((2, outer, 2, gp, D), BF16), vm((2, outer, gp, D), BF16),
            vm((2, outer, gp, D), BF16), vm((2, outer, gp, D), BF16),
            dma((5,)),
            dma((3, chips)), dma((3, chips)), dma((3,)), dma((3,)), dma((3, chips)), dma((3, chips)),
            dma((2,)), dma((2,)), dma((2, chips)), dma((2, chips)), dma((2, chips)), dma((2, chips)),
            dma((2, outer)), dma((2, outer)), dma((2, outer)), dma((2, outer)),
        ],
        compiler_params=pltpu.CompilerParams(collective_id=0, has_side_effects=True,
                                             vmem_limit_bytes=60 * 1024 * 1024),
        name="moe_layer",
    )(tokens, cotangent, expert_ids.T, gate_weights.T, w_gate, w_up, w_down)
    if not fused:
        gup = lax.psum_scatter(gup, "dp", scatter_dimension=0, tiled=True)
        gdn = lax.psum_scatter(gdn, "dp", scatter_dimension=0, tiled=True)
        return layer_out, grad_tokens, gup[None], gdn[None]
    results = [pltpu.with_memory_space_constraint(r, pltpu.VMEM) for r in (layer_out, grad_tokens, gup, gdn)]
    layer_out, grad_tokens, gup, gdn = pl.pallas_call(
        write_out,
        out_shape=tuple(jax.ShapeDtypeStruct(r.shape, r.dtype) for r in results),
        in_specs=[vspec] * 4,
        out_specs=(anyspec,) * 4,
        scratch_shapes=[dma((4,))],
        name="write_out",
    )(*results)
    return layer_out, grad_tokens, gup[None], gdn[None]


def solution(mesh):
    both = P(("dp", "expert"), None)
    weights = P("expert", None, None)
    return jax.shard_map(
        shards,
        mesh=mesh,
        in_specs=(both, both, both, both, weights, weights, weights),
        out_specs=(both, both, P("expert", "dp", None), P("expert", "dp", None)),
        check_vma=False,
    )
```

```python
import functools

import jax
import jax.numpy as jnp
from jax import lax
from jax.experimental import pallas as pl
from jax.experimental.pallas import tpu as pltpu
from jax.sharding import PartitionSpec as P

MESH = pl.DeviceIdType.MESH
F32 = jnp.float32
BF16 = jnp.bfloat16


def dot_nn(a, b):
    return lax.dot_general(a, b, (((1,), (0,)), ((), ())), preferred_element_type=F32)


def dot_nt(a, b):
    return lax.dot_general(a, b, (((1,), (1,)), ((), ())), preferred_element_type=F32)


def layer_kernel(cfg, tok_hbm, cot_hbm, ids_ref, gw_ref, wg_hbm, wu_hbm, wd_hbm,
                 out_ref, gtok_ref, gup_ref, gdn_ref,
                 wg, wu, wd, xb, cb, gates_ref, gts, gob, hT, guT, silu_s, q_s, ggp_s, gup_s,
                 part, pre, pre_send, ret, gbuf, yrecv, zsend, zrecv,
                 local_sem, xs, xr, ps, pr, rs, rr, ts, tr, qs, qr, us, ur, ys, yr, zs, zr):
    chips, outer, fused, scale = cfg
    T, D = tok_hbm.shape
    H = wg.shape[0]
    R2 = 2 * T
    dp = lax.axis_index("dp")
    ex = lax.axis_index("expert")
    core = lax.rem(ex, 2)
    chip = lax.div(ex, 2)
    partner = (dp, chip * 2 + 1 - core)

    def ahead(d):
        return (dp, lax.rem(chip + d, chips) * 2 + core)

    def behind(d):
        return (dp, lax.rem(chip + chips - d, chips) * 2 + core)

    yi = lax.rem(dp, 2)
    zo = lax.div(dp, 2)
    ypeer = (zo * 2 + 1 - yi, ex)

    levels = outer.bit_length() - 1

    def flipped(m):
        z = zo
        for b in range(levels):
            if (m >> b) & 1:
                z = z + (1 << b) * (1 - 2 * lax.rem(lax.div(zo, 1 << b), 2))
        return z

    def remote(src, dst, ssem, rsem, dev):
        return pltpu.make_async_remote_copy(src_ref=src, dst_ref=dst, send_sem=ssem, recv_sem=rsem,
                                            device_id=dev, device_id_type=MESH)

    locals_ = [
        pltpu.make_async_copy(tok_hbm, xb.at[0], local_sem.at[0]),
        pltpu.make_async_copy(wg_hbm.at[0], wg, local_sem.at[1]),
        pltpu.make_async_copy(wu_hbm.at[0], wu, local_sem.at[2]),
        pltpu.make_async_copy(wd_hbm.at[0], wd, local_sem.at[3]),
        pltpu.make_async_copy(cot_hbm, cb.at[0], local_sem.at[4]),
    ]
    for c in locals_:
        c.start()

    ranks = lax.broadcasted_iota(jnp.int32, gates_ref.shape, 0)
    table = jnp.zeros(gates_ref.shape, F32)
    for k in range(ids_ref.shape[0]):
        table = table + jnp.where(ids_ref[pl.ds(k, 1), :] == ranks, gw_ref[pl.ds(k, 1), :], 0.0)
    gates_ref[...] = table

    peers = [partner] + [ahead(d) for d in range(1, chips)]
    if fused:
        peers = peers + [ypeer] + [(flipped(1 << b) * 2 + yi, ex) for b in range(levels)]
    barrier = pltpu.get_barrier_semaphore()
    for dev in peers:
        pl.semaphore_signal(barrier, inc=1, device_id=dev, device_id_type=MESH)
    pl.semaphore_wait(barrier, len(peers))

    pending = []

    def go(c):
        c.start()
        pending.append(c)
        return c

    srcs = [gates_ref, tok_hbm, cot_hbm]
    bufs = [gts, xb, cb]
    xin, pin, rin = {}, {}, {}
    for t in range(3):
        for d in range(1, chips):
            xin[t, d] = go(remote(srcs[t], bufs[t].at[2 * d], xs.at[t, d], xr.at[t, d], ahead(d)))
        if t < 2:
            pin[t] = go(remote(srcs[t], bufs[t].at[1], ps.at[t], pr.at[t], partner))
    pin[2] = go(remote(srcs[2], bufs[2].at[1], ps.at[2], pr.at[2], partner))

    def relay(t):
        for d in range(1, chips):
            xin[t, d].wait_recv()
            rin[t, d] = go(remote(bufs[t].at[2 * d], bufs[t].at[2 * d + 1], rs.at[t, d], rr.at[t, d], partner))

    eye = lax.broadcasted_iota(jnp.int32, (T, T), 0) == lax.broadcasted_iota(jnp.int32, (T, T), 1)

    def gate_col(p):
        cols = []
        for s in (2 * p, 2 * p + 1):
            row = gates_ref[pl.ds(ex, 1), :] if s == 0 else gts[s, pl.ds(ex, 1), :]
            cols.append(jnp.sum(jnp.where(eye, row, 0.0), axis=1, keepdims=True))
        return jnp.concatenate(cols, axis=0)

    def forward(p):
        rows = pl.ds(p * R2, R2)
        x = xb[2 * p:2 * p + 2].reshape(R2, D)
        gp = dot_nt(x, wg[...])
        up = dot_nt(x, wu[...])
        sig = jax.nn.sigmoid(gp)
        silu = gp * sig
        hidden = (silu * up).astype(BF16)
        silu_s[rows, :] = silu
        q_s[rows, :] = up * sig * (1.0 + gp * (1.0 - sig))
        hT[:, rows] = hidden.T
        return hidden

    def forward_out(p, hidden):
        eo = gate_col(p) * dot_nn(hidden, wd[...])
        part[0, 2 * p:2 * p + 2] = eo.astype(BF16).reshape(2, T, D)

    def weighted(p):
        go_ = gate_col(p) * cb[2 * p:2 * p + 2].reshape(R2, D).astype(F32)
        gob[pl.ds(p * R2, R2), :] = go_.astype(BF16)

    def backward(p):
        rows = pl.ds(p * R2, R2)
        gh = dot_nt(gob[rows, :], wd[...])
        gu = (gh * silu_s[rows, :]).astype(BF16)
        gup_s[rows, :] = gu
        ggp_s[rows, :] = (gh * q_s[rows, :]).astype(BF16)
        guT[:, rows] = gu.T

    def backward_in(p):
        rows = pl.ds(p * R2, R2)
        gi = dot_nn(ggp_s[rows, :], wg[...]) + dot_nn(gup_s[rows, :], wu[...])
        part[1, 2 * p:2 * p + 2] = gi.astype(BF16).reshape(2, T, D)

    locals_[0].wait()
    locals_[1].wait()
    locals_[2].wait()
    pin[0].wait_recv()
    pin[1].wait_recv()
    hidden = forward(0)
    locals_[3].wait()
    forward_out(0, hidden)
    tin, qin, uin = {}, {}, {}
    tin[0] = go(remote(part.at[0, 1], ret.at[0, 0], ts.at[0], tr.at[0], partner))
    relay(0)
    locals_[4].wait()
    pin[2].wait_recv()
    weighted(0)
    backward(0)
    relay(1)
    backward_in(0)
    tin[1] = go(remote(part.at[1, 1], ret.at[1, 0], ts.at[1], tr.at[1], partner))

    def hand_over(k):
        for d in range(1, chips):
            qin[k, d] = go(remote(part.at[k, 2 * d + 1], pre.at[k, d], qs.at[k, d], qr.at[k, d], partner))

    def send_back(k):
        for d in range(1, chips):
            qin[k, d].wait_recv()
            pre_send[k, d] = (part[k, 2 * d].astype(F32) + pre[k, d].astype(F32)).astype(BF16)
            uin[k, d] = go(remote(pre_send.at[k, d], ret.at[k, d], us.at[k, d], ur.at[k, d], behind(d)))

    for d in range(1, chips):
        rin[0, d].wait_recv()
        rin[1, d].wait_recv()
        forward_out(d, forward(d))
    hand_over(0)
    relay(2)
    for d in range(1, chips):
        rin[2, d].wait_recv()
        weighted(d)

    yin, zin = {}, {}
    order = sorted(range(outer), key=lambda m: ((m & -m) if m else outer, -m))

    def weight_grad(k, left, right, full_ref):
        tile = 256 if D % 256 == 0 else D
        for n in range(D // tile):
            cols = pl.ds(n * tile, tile)
            g = dot_nn(left[...], right(cols))
            if fused:
                gbuf[k, :, :, :, cols] = g.astype(BF16).reshape(gbuf.shape[1:4] + (tile,))
            else:
                full_ref[:, cols] = g * scale
        if fused:
            for m in order:
                yin[k, m] = go(remote(gbuf.at[k, flipped(m), 1 - yi], yrecv.at[k, m],
                                      ys.at[k, m], yr.at[k, m], ypeer))

    def halve(k, b):
        for m in order:
            if (m & -m) == 1 << b:
                total = level_sum(k, m, b)
                zsend[k, m] = total.astype(BF16)
                zin[k, m] = go(remote(zsend.at[k, m], zrecv.at[k, m], zs.at[k, m], zr.at[k, m],
                                      (flipped(1 << b) * 2 + yi, ex)))

    def level_sum(k, m, b):
        yin[k, m].wait_recv()
        total = gbuf[k, flipped(m), yi].astype(F32) + yrecv[k, m].astype(F32)
        for a in range(b):
            zin[k, m + (1 << a)].wait_recv()
            total = total + zrecv[k, m + (1 << a)].astype(F32)
        return total

    def outer_end(k, ref):
        ref[...] = level_sum(k, 0, levels) * scale

    weight_grad(0, hT, lambda cols: gob[:, cols], gdn_ref)
    for d in range(1, chips):
        backward(d)
    weight_grad(1, guT, lambda cols: jnp.concatenate([xb[s, :, cols] for s in range(2 * chips)], axis=0), gup_ref)
    send_back(0)
    for d in range(1, chips):
        backward_in(d)
    hand_over(1)
    if fused and levels > 0:
        halve(0, 0)
    send_back(1)
    if fused:
        for b in range(1, levels):
            halve(0, b)
        for b in range(levels):
            halve(1, b)

    def collect(k, ref):
        total = part[k, 0].astype(F32)
        tin[k].wait_recv()
        total = total + ret[k, 0].astype(F32)
        for d in range(1, chips):
            uin[k, d].wait_recv()
            total = total + ret[k, d].astype(F32)
        ref[...] = total.astype(BF16)

    collect(0, out_ref)
    collect(1, gtok_ref)
    if fused:
        outer_end(0, gdn_ref)
        outer_end(1, gup_ref)
    for c in pending:
        c.wait_send()


def write_out(a, b, c, d, out_a, out_b, out_c, out_d, sem):
    copies = [pltpu.make_async_copy(src, dst, sem.at[i])
              for i, (src, dst) in enumerate([(a, out_a), (b, out_b), (c, out_c), (d, out_d)])]
    for c in copies:
        c.start()
    for c in copies:
        c.wait()


def shards(tokens, cotangent, expert_ids, gate_weights, w_gate, w_up, w_down):
    T, D = tokens.shape
    local_experts, H, _ = w_gate.shape
    groups = lax.axis_size("expert")
    dps = lax.axis_size("dp")
    experts = groups * local_experts
    assert local_experts == 1 and groups % 2 == 0
    chips = groups // 2
    piece = H // dps
    fused = dps % 2 == 0 and piece % 16 == 0 and (dps & (dps - 1)) == 0
    outer = dps // 2 if fused else 1
    top = expert_ids.shape[1]
    scale = (T * dps * groups * top / experts) ** (-0.5)
    erows = -(-experts // 8) * 8
    R = groups * T
    grad_shape = (piece, D) if fused else (H, D)
    gp = piece if fused else 16
    vm = pltpu.VMEM
    dma = pltpu.SemaphoreType.DMA
    anyspec = pl.BlockSpec(memory_space=pl.ANY)
    vspec = pl.BlockSpec(memory_space=pltpu.VMEM)
    layer_out, grad_tokens, gup, gdn = pl.pallas_call(
        functools.partial(layer_kernel, (chips, outer, fused, scale)),
        out_shape=(
            vm((T, D), BF16),
            vm((T, D), BF16),
            vm(grad_shape, F32),
            vm(grad_shape, F32),
        ),
        in_specs=[anyspec, anyspec, vspec, vspec, anyspec, anyspec, anyspec],
        out_specs=(vspec, vspec, vspec, vspec),
        scratch_shapes=[
            vm((H, D), BF16), vm((H, D), BF16), vm((H, D), BF16),
            vm((groups, T, D), BF16), vm((groups, T, D), BF16), vm((erows, T), F32), vm((groups, erows, T), F32),
            vm((R, D), BF16), vm((H, R), BF16), vm((H, R), BF16),
            vm((R, H), F32), vm((R, H), F32), vm((R, H), BF16), vm((R, H), BF16),
            vm((2, groups, T, D), BF16), vm((2, chips, T, D), BF16), vm((2, chips, T, D), BF16),
            vm((2, chips, T, D), BF16),
            vm((2, outer, 2, gp, D), BF16), vm((2, outer, gp, D), BF16),
            vm((2, outer, gp, D), BF16), vm((2, outer, gp, D), BF16),
            dma((5,)),
            dma((3, chips)), dma((3, chips)), dma((3,)), dma((3,)), dma((3, chips)), dma((3, chips)),
            dma((2,)), dma((2,)), dma((2, chips)), dma((2, chips)), dma((2, chips)), dma((2, chips)),
            dma((2, outer)), dma((2, outer)), dma((2, outer)), dma((2, outer)),
        ],
        compiler_params=pltpu.CompilerParams(collective_id=0, has_side_effects=True,
                                             vmem_limit_bytes=60 * 1024 * 1024),
        name="moe_layer",
    )(tokens, cotangent, expert_ids.T, gate_weights.T, w_gate, w_up, w_down)
    if not fused:
        gup = lax.psum_scatter(gup, "dp", scatter_dimension=0, tiled=True)
        gdn = lax.psum_scatter(gdn, "dp", scatter_dimension=0, tiled=True)
        return layer_out, grad_tokens, gup[None], gdn[None]
    results = [pltpu.with_memory_space_constraint(r, pltpu.VMEM) for r in (layer_out, grad_tokens, gup, gdn)]
    layer_out, grad_tokens, gup, gdn = pl.pallas_call(
        write_out,
        out_shape=tuple(jax.ShapeDtypeStruct(r.shape, r.dtype) for r in results),
        in_specs=[vspec] * 4,
        out_specs=(anyspec,) * 4,
        scratch_shapes=[dma((4,))],
        name="write_out",
    )(*results)
    return layer_out, grad_tokens, gup[None], gdn[None]


def solution(mesh):
    both = P(("dp", "expert"), None)
    weights = P("expert", None, None)
    return jax.shard_map(
        shards,
        mesh=mesh,
        in_specs=(both, both, both, both, weights, weights, weights),
        out_specs=(both, both, P("expert", "dp", None), P("expert", "dp", None)),
        check_vma=False,
    )
```

```python
import functools

import jax
import jax.numpy as jnp
from jax import lax
from jax.experimental import pallas as pl
from jax.experimental.pallas import tpu as pltpu
from jax.sharding import PartitionSpec as P

MESH = pl.DeviceIdType.MESH
F32 = jnp.float32
BF16 = jnp.bfloat16


def dot_nn(a, b):
    return lax.dot_general(a, b, (((1,), (0,)), ((), ())), preferred_element_type=F32)


def dot_nt(a, b):
    return lax.dot_general(a, b, (((1,), (1,)), ((), ())), preferred_element_type=F32)


def layer_kernel(cfg, tok_hbm, cot_hbm, ids_ref, gw_ref, wg_hbm, wu_hbm, wd_hbm,
                 out_ref, gtok_ref, gup_ref, gdn_ref,
                 wg, wu, wd, xb, cb, gates_ref, gts, gob, hT, guT, silu_s, q_s, ggp_s, gup_s,
                 part, pre, pre_send, ret, gbuf, yrecv, zsend, zrecv,
                 local_sem, xs, xr, ps, pr, rs, rr, ts, tr, qs, qr, us, ur, ys, yr, zs, zr):
    chips, outer, fused, scale = cfg
    T, D = tok_hbm.shape
    H = wg.shape[0]
    R2 = 2 * T
    dp = lax.axis_index("dp")
    ex = lax.axis_index("expert")
    core = lax.rem(ex, 2)
    chip = lax.div(ex, 2)
    partner = (dp, chip * 2 + 1 - core)

    def ahead(d):
        return (dp, lax.rem(chip + d, chips) * 2 + core)

    def behind(d):
        return (dp, lax.rem(chip + chips - d, chips) * 2 + core)

    yi = lax.rem(dp, 2)
    zo = lax.div(dp, 2)
    ypeer = (zo * 2 + 1 - yi, ex)

    levels = outer.bit_length() - 1

    def flipped(m):
        z = zo
        for b in range(levels):
            if (m >> b) & 1:
                z = z + (1 << b) * (1 - 2 * lax.rem(lax.div(zo, 1 << b), 2))
        return z

    def remote(src, dst, ssem, rsem, dev):
        return pltpu.make_async_remote_copy(src_ref=src, dst_ref=dst, send_sem=ssem, recv_sem=rsem,
                                            device_id=dev, device_id_type=MESH)

    locals_ = [
        pltpu.make_async_copy(tok_hbm, xb.at[0], local_sem.at[0]),
        pltpu.make_async_copy(wg_hbm.at[0], wg, local_sem.at[1]),
        pltpu.make_async_copy(wu_hbm.at[0], wu, local_sem.at[2]),
        pltpu.make_async_copy(wd_hbm.at[0], wd, local_sem.at[3]),
        pltpu.make_async_copy(cot_hbm, cb.at[0], local_sem.at[4]),
    ]
    for c in locals_:
        c.start()

    ranks = lax.broadcasted_iota(jnp.int32, gates_ref.shape, 0)
    table = jnp.zeros(gates_ref.shape, F32)
    for k in range(ids_ref.shape[0]):
        table = table + jnp.where(ids_ref[pl.ds(k, 1), :] == ranks, gw_ref[pl.ds(k, 1), :], 0.0)
    gates_ref[...] = table

    peers = [partner] + [ahead(d) for d in range(1, chips)]
    if fused:
        peers = peers + [ypeer] + [(flipped(1 << b) * 2 + yi, ex) for b in range(levels)]
    barrier = pltpu.get_barrier_semaphore()
    for dev in peers:
        pl.semaphore_signal(barrier, inc=1, device_id=dev, device_id_type=MESH)
    pl.semaphore_wait(barrier, len(peers))

    pending = []

    def go(c):
        c.start()
        pending.append(c)
        return c

    srcs = [gates_ref, tok_hbm, cot_hbm]
    bufs = [gts, xb, cb]
    xin, pin, rin = {}, {}, {}
    for t in range(3):
        for d in range(1, chips):
            xin[t, d] = go(remote(srcs[t], bufs[t].at[2 * d], xs.at[t, d], xr.at[t, d], ahead(d)))
        if t < 2:
            pin[t] = go(remote(srcs[t], bufs[t].at[1], ps.at[t], pr.at[t], partner))
    pin[2] = go(remote(srcs[2], bufs[2].at[1], ps.at[2], pr.at[2], partner))

    def relay(t):
        for d in range(1, chips):
            xin[t, d].wait_recv()
            rin[t, d] = go(remote(bufs[t].at[2 * d], bufs[t].at[2 * d + 1], rs.at[t, d], rr.at[t, d], partner))

    eye = lax.broadcasted_iota(jnp.int32, (T, T), 0) == lax.broadcasted_iota(jnp.int32, (T, T), 1)

    def gate_col(p):
        cols = []
        for s in (2 * p, 2 * p + 1):
            row = gates_ref[pl.ds(ex, 1), :] if s == 0 else gts[s, pl.ds(ex, 1), :]
            cols.append(jnp.sum(jnp.where(eye, row, 0.0), axis=1, keepdims=True))
        return jnp.concatenate(cols, axis=0)

    def forward(p):
        rows = pl.ds(p * R2, R2)
        x = xb[2 * p:2 * p + 2].reshape(R2, D)
        gp = dot_nt(x, wg[...])
        up = dot_nt(x, wu[...])
        sig = jax.nn.sigmoid(gp)
        silu = gp * sig
        hidden = (silu * up).astype(BF16)
        silu_s[rows, :] = silu
        q_s[rows, :] = up * sig * (1.0 + gp * (1.0 - sig))
        hT[:, rows] = hidden.T
        return hidden

    def forward_out(p, hidden):
        eo = gate_col(p) * dot_nn(hidden, wd[...])
        part[0, 2 * p:2 * p + 2] = eo.astype(BF16).reshape(2, T, D)

    def weighted(p):
        go_ = gate_col(p) * cb[2 * p:2 * p + 2].reshape(R2, D).astype(F32)
        gob[pl.ds(p * R2, R2), :] = go_.astype(BF16)

    def backward(p):
        rows = pl.ds(p * R2, R2)
        gh = dot_nt(gob[rows, :], wd[...])
        gu = (gh * silu_s[rows, :]).astype(BF16)
        gup_s[rows, :] = gu
        ggp_s[rows, :] = (gh * q_s[rows, :]).astype(BF16)
        guT[:, rows] = gu.T

    def backward_in(p):
        rows = pl.ds(p * R2, R2)
        gi = dot_nn(ggp_s[rows, :], wg[...]) + dot_nn(gup_s[rows, :], wu[...])
        part[1, 2 * p:2 * p + 2] = gi.astype(BF16).reshape(2, T, D)

    locals_[0].wait()
    locals_[1].wait()
    locals_[2].wait()
    pin[0].wait_recv()
    pin[1].wait_recv()
    hidden = forward(0)
    locals_[3].wait()
    forward_out(0, hidden)
    tin, qin, uin = {}, {}, {}
    tin[0] = go(remote(part.at[0, 1], ret.at[0, 0], ts.at[0], tr.at[0], partner))
    relay(0)
    locals_[4].wait()
    pin[2].wait_recv()
    weighted(0)
    backward(0)
    relay(1)
    backward_in(0)
    tin[1] = go(remote(part.at[1, 1], ret.at[1, 0], ts.at[1], tr.at[1], partner))

    def hand_over(k):
        for d in range(1, chips):
            qin[k, d] = go(remote(part.at[k, 2 * d + 1], pre.at[k, d], qs.at[k, d], qr.at[k, d], partner))

    def send_back(k):
        for d in range(1, chips):
            qin[k, d].wait_recv()
            pre_send[k, d] = (part[k, 2 * d].astype(F32) + pre[k, d].astype(F32)).astype(BF16)
            uin[k, d] = go(remote(pre_send.at[k, d], ret.at[k, d], us.at[k, d], ur.at[k, d], behind(d)))

    for d in range(1, chips):
        rin[0, d].wait_recv()
        rin[1, d].wait_recv()
        forward_out(d, forward(d))
    hand_over(0)
    relay(2)
    for d in range(1, chips):
        rin[2, d].wait_recv()
        weighted(d)

    yin, zin = {}, {}
    order = sorted(range(outer), key=lambda m: ((m & -m) if m else outer, -m))

    def weight_grad(k, left, right, full_ref):
        tile = 256 if D % 256 == 0 else D
        for n in range(D // tile):
            cols = pl.ds(n * tile, tile)
            g = dot_nn(left[...], right(cols))
            if fused:
                gbuf[k, :, :, :, cols] = g.astype(BF16).reshape(gbuf.shape[1:4] + (tile,))
            else:
                full_ref[:, cols] = g * scale
        if fused:
            for j, m in [(k, m) for m in order[:-1]] + [(0, 0), (1, 0)] * k:
                yin[j, m] = go(remote(gbuf.at[j, flipped(m), 1 - yi], yrecv.at[j, m],
                                      ys.at[j, m], yr.at[j, m], ypeer))

    def halve(k, b):
        for m in order:
            if (m & -m) == 1 << b:
                total = level_sum(k, m, b)
                zsend[k, m] = total.astype(BF16)
                zin[k, m] = go(remote(zsend.at[k, m], zrecv.at[k, m], zs.at[k, m], zr.at[k, m],
                                      (flipped(1 << b) * 2 + yi, ex)))

    def level_sum(k, m, b):
        yin[k, m].wait_recv()
        total = gbuf[k, flipped(m), yi].astype(F32) + yrecv[k, m].astype(F32)
        for a in range(b):
            zin[k, m + (1 << a)].wait_recv()
            total = total + zrecv[k, m + (1 << a)].astype(F32)
        return total

    def outer_end(k, ref):
        ref[...] = level_sum(k, 0, levels) * scale

    weight_grad(0, hT, lambda cols: gob[:, cols], gdn_ref)
    for d in range(1, chips):
        backward(d)
    weight_grad(1, guT, lambda cols: jnp.concatenate([xb[s, :, cols] for s in range(2 * chips)], axis=0), gup_ref)
    send_back(0)
    for d in range(1, chips):
        backward_in(d)
    hand_over(1)
    if fused and levels > 0:
        halve(0, 0)
    send_back(1)
    if fused:
        for b in range(1, levels):
            halve(0, b)
        for b in range(levels):
            halve(1, b)

    def collect(k, ref):
        total = part[k, 0].astype(F32)
        tin[k].wait_recv()
        total = total + ret[k, 0].astype(F32)
        for d in range(1, chips):
            uin[k, d].wait_recv()
            total = total + ret[k, d].astype(F32)
        ref[...] = total.astype(BF16)

    collect(0, out_ref)
    collect(1, gtok_ref)
    if fused:
        outer_end(0, gdn_ref)
        outer_end(1, gup_ref)
    for c in pending:
        c.wait_send()


def write_out(a, b, c, d, out_a, out_b, out_c, out_d, sem):
    copies = [pltpu.make_async_copy(src, dst, sem.at[i])
              for i, (src, dst) in enumerate([(a, out_a), (b, out_b), (c, out_c), (d, out_d)])]
    for c in copies:
        c.start()
    for c in copies:
        c.wait()


def shards(tokens, cotangent, expert_ids, gate_weights, w_gate, w_up, w_down):
    T, D = tokens.shape
    local_experts, H, _ = w_gate.shape
    groups = lax.axis_size("expert")
    dps = lax.axis_size("dp")
    experts = groups * local_experts
    assert local_experts == 1 and groups % 2 == 0
    chips = groups // 2
    piece = H // dps
    fused = dps % 2 == 0 and piece % 16 == 0 and (dps & (dps - 1)) == 0
    outer = dps // 2 if fused else 1
    top = expert_ids.shape[1]
    scale = (T * dps * groups * top / experts) ** (-0.5)
    erows = -(-experts // 8) * 8
    R = groups * T
    grad_shape = (piece, D) if fused else (H, D)
    gp = piece if fused else 16
    vm = pltpu.VMEM
    dma = pltpu.SemaphoreType.DMA
    anyspec = pl.BlockSpec(memory_space=pl.ANY)
    vspec = pl.BlockSpec(memory_space=pltpu.VMEM)
    layer_out, grad_tokens, gup, gdn = pl.pallas_call(
        functools.partial(layer_kernel, (chips, outer, fused, scale)),
        out_shape=(
            vm((T, D), BF16),
            vm((T, D), BF16),
            vm(grad_shape, F32),
            vm(grad_shape, F32),
        ),
        in_specs=[anyspec, anyspec, vspec, vspec, anyspec, anyspec, anyspec],
        out_specs=(vspec, vspec, vspec, vspec),
        scratch_shapes=[
            vm((H, D), BF16), vm((H, D), BF16), vm((H, D), BF16),
            vm((groups, T, D), BF16), vm((groups, T, D), BF16), vm((erows, T), F32), vm((groups, erows, T), F32),
            vm((R, D), BF16), vm((H, R), BF16), vm((H, R), BF16),
            vm((R, H), F32), vm((R, H), F32), vm((R, H), BF16), vm((R, H), BF16),
            vm((2, groups, T, D), BF16), vm((2, chips, T, D), BF16), vm((2, chips, T, D), BF16),
            vm((2, chips, T, D), BF16),
            vm((2, outer, 2, gp, D), BF16), vm((2, outer, gp, D), BF16),
            vm((2, outer, gp, D), BF16), vm((2, outer, gp, D), BF16),
            dma((5,)),
            dma((3, chips)), dma((3, chips)), dma((3,)), dma((3,)), dma((3, chips)), dma((3, chips)),
            dma((2,)), dma((2,)), dma((2, chips)), dma((2, chips)), dma((2, chips)), dma((2, chips)),
            dma((2, outer)), dma((2, outer)), dma((2, outer)), dma((2, outer)),
        ],
        compiler_params=pltpu.CompilerParams(collective_id=0, has_side_effects=True,
                                             vmem_limit_bytes=60 * 1024 * 1024),
        name="moe_layer",
    )(tokens, cotangent, expert_ids.T, gate_weights.T, w_gate, w_up, w_down)
    if not fused:
        gup = lax.psum_scatter(gup, "dp", scatter_dimension=0, tiled=True)
        gdn = lax.psum_scatter(gdn, "dp", scatter_dimension=0, tiled=True)
        return layer_out, grad_tokens, gup[None], gdn[None]
    results = [pltpu.with_memory_space_constraint(r, pltpu.VMEM) for r in (layer_out, grad_tokens, gup, gdn)]
    layer_out, grad_tokens, gup, gdn = pl.pallas_call(
        write_out,
        out_shape=tuple(jax.ShapeDtypeStruct(r.shape, r.dtype) for r in results),
        in_specs=[vspec] * 4,
        out_specs=(anyspec,) * 4,
        scratch_shapes=[dma((4,))],
        name="write_out",
    )(*results)
    return layer_out, grad_tokens, gup[None], gdn[None]


def solution(mesh):
    both = P(("dp", "expert"), None)
    weights = P("expert", None, None)
    return jax.shard_map(
        shards,
        mesh=mesh,
        in_specs=(both, both, both, both, weights, weights, weights),
        out_specs=(both, both, P("expert", "dp", None), P("expert", "dp", None)),
        check_vma=False,
    )
```
